32 devices in a mesh: fsdp: 4 (over y, x), ctx: 8 (over z, core).
Axes of the slice: x: 2, y: 2, z: 4, core: 2. Of those that a mesh axis runs over, the one named last changes fastest.
Arguments:
- tokens: bfloat16 [2, 4, 1024, 2048], P(None, 'fsdp', 'ctx'), may hold values from -6 to 6
- out_grad: bfloat16 [2, 4, 1024, 2048], P(None, 'fsdp', 'ctx'), may hold values from -6 to 6
- doc_lengths: int32 [2, 4, 6], P(None, 'fsdp'), may hold values from 1 to 512, 1024 in all within a row
- routes: int32 [2, 4, 1024, 8], P(None, 'fsdp', 'ctx'), may hold values from 0 to 63, as said below
- gate_values: float32 [2, 4, 1024, 8], P(None, 'fsdp', 'ctx'), may hold values from 0.25 to 1
- attn_gain: bfloat16 [2048], P('fsdp'), may hold values from 0.5 to 1.5
- w_query: bfloat16 [2048, 2048], P('fsdp'), may hold values from -0.125 to 0.125
- w_key: bfloat16 [2048, 2048], P('fsdp'), may hold values from -0.125 to 0.125
- w_value: bfloat16 [2048, 2048], P('fsdp'), may hold values from -0.125 to 0.125
- w_out: bfloat16 [2048, 2048], P('fsdp'), may hold values from -1 to 1
- query_gain: bfloat16 [128], P('fsdp'), may hold values from 0.5 to 1.5
- key_gain: bfloat16 [128], P('fsdp'), may hold values from 0.5 to 1.5
- ffn_gain: bfloat16 [2048], P('fsdp'), may hold values from 0.5 to 1.5
- w_gate: bfloat16 [1, 2048, 1024], P(None, 'fsdp'), may hold values from -0.125 to 0.125
- w_up: bfloat16 [1, 2048, 1024], P(None, 'fsdp'), may hold values from -0.125 to 0.125
- w_down: bfloat16 [1, 1024, 2048], P(None, 'fsdp'), may hold values from -0.1875 to 0.1875
Outputs:
- mixed_out: bfloat16 [2, 4, 1024, 2048], P(None, 'fsdp', 'ctx')
- tokens_grad: float32 [2, 4, 1024, 2048], P(None, 'fsdp', 'ctx')
- attn_gain_grad: float32 [2048], P('fsdp')
- w_query_grad: float32 [2048, 2048], P('fsdp')
- w_key_grad: float32 [2048, 2048], P('fsdp')
- w_value_grad: float32 [2048, 2048], P('fsdp')
- w_out_grad: float32 [2048, 2048], P('fsdp')
- query_gain_grad: float32 [128], P('fsdp')
- key_gain_grad: float32 [128], P('fsdp')
- ffn_gain_grad: float32 [2048], P('fsdp')
- w_gate_grad: float32 [1, 2048, 1024], P(None, 'fsdp')
- w_up_grad: float32 [1, 2048, 1024], P(None, 'fsdp')
- w_down_grad: float32 [1, 1024, 2048], P(None, 'fsdp')
The draws below stay inside these ranges and needn't reach their ends.
Inputs may be any that keep to these rules, and one draw needn't show every extreme that they name: `routes`: each row names 8 different experts. Within one micro-batch, the 128 rows of one stream on one device name expert e, for each e below 1, in 16 to 32 rows, and for each such e, exactly 32 rows on one device of the whole draw. `doc_lengths`: the lengths of a stream sum to 1024.
All inputs are finite; a program needn't handle non-finite values.
Results may differ from the reference program's by a relative error of at most 0.023.
Values may be sent and summed in bfloat16 or wider, within the bound.
No kernel may reach another device: no remote copies, remote signals or barrier semaphores. Data moves between devices by JAX's collectives and lax.ppermute only.
A program may use at most 384 MiB of HBM per device.

```python
import math
import jax
import jax.numpy as jnp
import numpy as np
from jax import lax

D = 2048
HEADS = 16
HD = 128
FF = 1024
EXPERTS = 64
TOPK = 8
EXP_WIN = 1
MICRO = 2
DOCS = 6
TOK_DEV = 128
SEQ = 1024
STREAMS = 4
CAP = 32


def draw_routes(key, part):
    block_count = MICRO * STREAMS * (SEQ // TOK_DEV)
    count_key = jax.random.fold_in(key, 11)
    pick_key = jax.random.fold_in(key, 12)
    order_key = jax.random.fold_in(key, 13)
    other_key = jax.random.fold_in(key, 14)
    shuffle_key = jax.random.fold_in(key, 15)
    counts = jax.random.randint(count_key, (block_count, EXP_WIN), CAP - CAP // 2, CAP + 1)
    picked = jax.random.randint(pick_key, (EXP_WIN,), 0, block_count)
    counts = jnp.where(jnp.arange(block_count)[:, None] == picked[None, :], CAP, counts)
    order_scores = jax.random.randint(order_key, (block_count, EXP_WIN, TOK_DEV), 0, 1 << 16) * TOK_DEV + jnp.arange(TOK_DEV)
    rank_rows = jnp.argsort(jnp.argsort(order_scores, axis=-1, stable=True), axis=-1, stable=True)
    members = jnp.transpose(rank_rows < counts[:, :, None], (0, 2, 1))
    padding = jnp.zeros((block_count, TOK_DEV, EXPERTS - EXP_WIN), dtype=bool)
    members = jnp.concatenate([members, padding], axis=-1)
    other_scores = jax.random.randint(other_key, (block_count, TOK_DEV, EXPERTS), 0, 1 << 16) * EXPERTS + jnp.arange(EXPERTS)
    window = jnp.arange(EXPERTS) < EXP_WIN
    scores = jnp.where(window, jnp.where(members, 1 << 30, -1), other_scores).astype(jnp.int32)
    picked_scores, chosen = lax.top_k(scores, TOPK)
    shuffle = jax.random.randint(shuffle_key, (block_count, TOK_DEV, TOPK), 0, 1 << 16) * TOPK + jnp.arange(TOPK)
    reorder = jnp.argsort(shuffle, axis=-1, stable=True)
    routed = jnp.take_along_axis(chosen, reorder, axis=-1)
    return routed.reshape(MICRO, STREAMS, SEQ, TOPK).astype(jnp.int32)


def steps_of(stream_key, dims, split, low, high):
    level, own = 1.0, jax.random.fold_in(stream_key, 6)
    for axis_at, blocks in split:
        steps = jnp.exp(jax.random.uniform(jax.random.fold_in(own, axis_at), (blocks,), jnp.float32, low / len(split), high / len(split)))
        level = level * jnp.repeat(steps, dims[axis_at] // blocks).reshape([-1 if axis == axis_at else 1 for axis in range(len(dims))])
    return level


def length_profile(count, total, limit, lean):
    weights = [(1 << 20) // math.isqrt(standing ** lean) + 1 for standing in range(2, count + 1)]
    rest, given = total - limit - (count - 1), [1] * (count - 1)
    while rest > 0:
        free = [i for i in range(count - 1) if given[i] < limit]
        whole, left = sum([weights[i] for i in free]), rest
        for i in free:
            more = min(limit - given[i], max(1, left * weights[i] // whole), rest)
            given[i] = given[i] + more
            rest = rest - more
    return np.array([limit] + given)


def uneven_parts(stream_key, count, total, most, lean):
    if count == 2:
        one = jax.random.randint(stream_key, (), max(1, total - most), min(most, total - 1) + 1)
        return jnp.stack([one, total - one])
    tallies = jnp.asarray(length_profile(count, total, most, lean), jnp.int32)
    twos = (count - 1) // 2
    source_of, sink = tallies[1:1 + 2 * twos:2], tallies[2:2 + 2 * twos:2]
    room = jnp.minimum(source_of - 1, most - sink)
    shifted = jax.random.randint(jax.random.fold_in(stream_key, 1), (twos,), 0, 1 << 20) % (room + 1)
    tallies = tallies.at[1:1 + 2 * twos:2].set(source_of - shifted).at[2:2 + 2 * twos:2].set(sink + shifted)
    return tallies[jax.random.permutation(jax.random.fold_in(stream_key, 2), count)]


def bell_draw(stream_key, shape, scale, limit, split=(), kind=jnp.bfloat16):
    drawn = jax.random.normal(stream_key, shape, jnp.float32) * scale
    if len(split) > 0:
        drawn = steps_of(stream_key, shape, split, -0.22, 0.18) * drawn
    return jnp.clip(drawn, min=-limit, max=limit).astype(kind)


def setup_inputs(seed: int = 0) -> dict:
    seeds = jax.random.split(jax.random.key(seed), 17)
    tokens = bell_draw(seeds[0], (MICRO, STREAMS, SEQ, D), 1.0, 6.0, ((1, 4), (2, 8)))
    out_grad = bell_draw(seeds[1], (MICRO, STREAMS, SEQ, D), 1.0, 6.0, ((1, 4), (2, 8)))
    doc_lengths = jax.vmap(lambda own: uneven_parts(own, DOCS, SEQ, SEQ // 2, 2))(jax.random.split(seeds[2], MICRO * STREAMS)).reshape((MICRO, STREAMS, DOCS)).astype(jnp.int32)
    routes = draw_routes(jax.random.fold_in(seeds[16], 71), 0)
    gate_values = jnp.clip(0.25 + 0.75 * jax.random.uniform(seeds[4], (MICRO, STREAMS, SEQ, TOPK), jnp.float32) ** steps_of(seeds[4], (MICRO, STREAMS, SEQ, TOPK), ((1, 4), (2, 8)), -0.2, 0.2), 0.25, 1.0)
    attn_gain = jnp.clip(1.0 + 0.1 * jax.random.normal(seeds[5], (D,), jnp.float32), 0.5, 1.5).astype(jnp.bfloat16)
    w_query = bell_draw(seeds[6], (D, D), D ** -0.5, 0.125, ((0, 4),))
    w_key = bell_draw(seeds[7], (D, D), D ** -0.5, 0.125, ((0, 4),))
    w_value = bell_draw(seeds[8], (D, D), D ** -0.5, 0.125, ((0, 4),))
    w_out = bell_draw(seeds[9], (D, D), (D // 64) ** -0.5, 1.0, ((0, 4),))
    query_gain = jnp.clip(1.0 + 0.1 * jax.random.normal(seeds[10], (HD,), jnp.float32), 0.5, 1.5).astype(jnp.bfloat16)
    key_gain = jnp.clip(1.0 + 0.1 * jax.random.normal(seeds[11], (HD,), jnp.float32), 0.5, 1.5).astype(jnp.bfloat16)
    ffn_gain = jnp.clip(1.0 + 0.1 * jax.random.normal(seeds[12], (D,), jnp.float32), 0.5, 1.5).astype(jnp.bfloat16)
    w_gate = bell_draw(seeds[13], (EXP_WIN, D, FF), D ** -0.5, 0.125, ((1, 4),))
    w_up = bell_draw(seeds[14], (EXP_WIN, D, FF), D ** -0.5, 0.125, ((1, 4),))
    w_down = bell_draw(seeds[15], (EXP_WIN, FF, D), FF ** -0.5, 0.1875, ((1, 4),))
    return dict(tokens=tokens, out_grad=out_grad, doc_lengths=doc_lengths, routes=routes, gate_values=gate_values, attn_gain=attn_gain, w_query=w_query, w_key=w_key, w_value=w_value, w_out=w_out, query_gain=query_gain, key_gain=key_gain, ffn_gain=ffn_gain, w_gate=w_gate, w_up=w_up, w_down=w_down)


@jax.custom_vjp
def low(v):
    return lax.optimization_barrier(v.astype(jnp.bfloat16)).astype(jnp.float32)

@jax.custom_vjp
def low_back(v):
    return v

def low_keep(v):
    return (low(v), None)

def low_pass(kept, grad):
    return (grad,)

def back_keep(v):
    return (v, None)

def back_low(kept, grad):
    return (low(grad),)
low.defvjp(low_keep, low_pass)
low_back.defvjp(back_keep, back_low)
EPS = 1e-06
ROPE_BASE = 50000.0
HIGHEST = lax.Precision.HIGHEST

def rms_gain(values, gain_row):
    return values * lax.rsqrt(lax.optimization_barrier(jnp.mean(values * values, axis=-1, keepdims=True)) + EPS) * gain_row

def rope_tables(positions, rope_width):
    half_width = rope_width // 2
    inverse = ROPE_BASE ** (-jnp.arange(half_width, dtype=jnp.float32) / half_width)
    angles = positions.astype(jnp.float32)[:, None] * inverse[None, :]
    return (jnp.cos(angles), jnp.sin(angles))

def rotate(values, cosine, sinusoid):
    half_width = values.shape[-1] // 2
    first_half = values[..., :half_width]
    second_half = values[..., half_width:]
    cos_rows = cosine[:, None, :]
    sin_rows = sinusoid[:, None, :]
    return jnp.concatenate([first_half * cos_rows - second_half * sin_rows, second_half * cos_rows + first_half * sin_rows], axis=-1)

def doc_info(lengths, positions):
    doc_ends = jnp.cumsum(lengths).astype(jnp.int32)
    passed = (doc_ends[None, :] <= positions[:, None]).astype(jnp.int32)
    doc_ids = lax.optimization_barrier(jnp.sum(passed, axis=1)).astype(jnp.int32)
    starts = lax.optimization_barrier(jnp.sum(passed * lengths[None, :], axis=1)).astype(jnp.int32)
    return (doc_ids, positions - starts)

def attend_block(queries, query_docs, key_rows, values, key_docs):
    scores = jnp.einsum('qhd,khd->hqk', queries, key_rows, precision=HIGHEST) * HD ** (-0.5)
    inside = (query_docs[:, None] == key_docs[None, :])[None]
    scores = low_back(jnp.where(inside, scores, -1e+30))
    chances = low(jax.nn.softmax(scores, axis=-1))
    return jnp.einsum('hqk,khd->qhd', chances, values, precision=HIGHEST)

def layer_forward(inputs, attn_gain, w_query, w_key, w_value, w_out, query_gain, key_gain, ffn_gain, w_gate, w_up, w_down, weights_in, doc_ids, offsets):
    length = inputs.shape[0]
    normed = low(rms_gain(inputs, attn_gain))
    raw_query = low_back(jnp.dot(normed, w_query, precision=HIGHEST))
    raw_key = low_back(jnp.dot(normed, w_key, precision=HIGHEST))
    raw_value = low_back(jnp.dot(normed, w_value, precision=HIGHEST))
    cosine, sinusoid = rope_tables(offsets, HD)
    queries = low(rotate(rms_gain(raw_query.reshape(length, HEADS, HD), query_gain), cosine, sinusoid))
    key_rows = low(rotate(rms_gain(raw_key.reshape(length, HEADS, HD), key_gain), cosine, sinusoid))
    values = low(raw_value).reshape(length, HEADS, HD)
    block_size = min(512, length)
    block_count = length // block_size

    def one_block(block_pair):
        return jax.checkpoint(attend_block)(block_pair[0], block_pair[1], key_rows, values, doc_ids)
    attended = lax.map(one_block, (queries.reshape(block_count, block_size, HEADS, HD), doc_ids.reshape(block_count, block_size)))
    mixed_heads = low(low_back(attended.reshape(length, D)))
    branch = low_back(jnp.dot(mixed_heads, w_out, precision=HIGHEST))
    hidden = inputs + branch
    ffn_in = low(rms_gain(hidden, ffn_gain))
    result = hidden
    for expert in range(EXP_WIN):
        gate_act = low_back(jnp.dot(ffn_in, w_gate[expert], precision=HIGHEST))
        upward = low_back(jnp.dot(ffn_in, w_up[expert], precision=HIGHEST))
        inner_act = low(jax.nn.silu(gate_act) * upward)
        expert_out = low_back(jnp.dot(inner_act, w_down[expert], precision=HIGHEST))
        result = result + weights_in[:, expert:expert + 1] * expert_out
    return result

def reference(tokens, out_grad, doc_lengths, routes, gate_values, attn_gain, w_query, w_key, w_value, w_out, query_gain, key_gain, ffn_gain, w_gate, w_up, w_down):
    params = tuple((weight.astype(jnp.float32) for weight in (attn_gain, w_query, w_key, w_value, w_out, query_gain, key_gain, ffn_gain, w_gate, w_up, w_down)))
    sequences = MICRO * STREAMS
    flat_tokens = tokens.reshape(sequences, SEQ, D)
    flat_grads = out_grad.reshape(sequences, SEQ, D)
    flat_lengths = doc_lengths.reshape(sequences, DOCS)
    flat_routes = routes.reshape(sequences, SEQ, TOPK)
    flat_gates = gate_values.reshape(sequences, SEQ, TOPK)
    positions = jnp.arange(SEQ, dtype=jnp.int32)

    def one_sequence(totals, element):
        seq_tokens, seq_grad, seq_lengths, seq_routes, seq_gates = element
        doc_ids, offsets = doc_info(seq_lengths, positions)
        weights_in = jnp.stack([lax.optimization_barrier(jnp.sum(jnp.where(seq_routes == expert, seq_gates, 0.0), axis=1)) for expert in range(EXP_WIN)], axis=1)

        def apply_layer(inputs, *weights):
            return layer_forward(inputs, *weights, weights_in, doc_ids, offsets)
        output, pullback = jax.vjp(apply_layer, seq_tokens.astype(jnp.float32), *params)
        gradients = pullback(seq_grad.astype(jnp.float32))
        summed = tuple((total + grad_part for total, grad_part in zip(totals, gradients[1:])))
        return (summed, (output.astype(jnp.bfloat16), gradients[0]))
    starting = tuple((jnp.zeros_like(weight) for weight in params))
    totals, (outputs, input_grads) = lax.scan(one_sequence, starting, (flat_tokens, flat_grads, flat_lengths, flat_routes, flat_gates))
    return (outputs.reshape(tokens.shape), input_grads.reshape(tokens.shape), totals[0], totals[1], totals[2], totals[3], totals[4], totals[5], totals[6], totals[7], totals[8], totals[9], totals[10])
```

```python
from functools import partial

import jax
import jax.numpy as jnp
from jax import lax
from jax.experimental import pallas as pl
from jax.experimental.pallas import tpu as pltpu
from jax.sharding import PartitionSpec as P

D = 2048
HEADS = 16
HD = 128
CAP = 32
EPS = 1e-06
ROPE_BASE = 50000.0
SCALE = HD ** (-0.5)
NEG = -1e30
BF = jnp.bfloat16
F32 = jnp.float32


def zshift(x, k):
    size = lax.axis_size("ctx")
    half = size // 2
    return lax.ppermute(x, "ctx", [(i, ((i // 2 + k) % half) * 2 + i % 2) for i in range(size)])


def swap(x):
    size = lax.axis_size("ctx")
    return lax.ppermute(x, "ctx", [(i, i ^ 1) for i in range(size)])


def fx(x, k):
    size = lax.axis_size("fsdp")
    return lax.ppermute(x, "fsdp", [(i, i ^ k) for i in range(size)])


def zring(x):
    got = [x]
    for _ in range(lax.axis_size("ctx") // 2 - 1):
        got.append(zshift(got[-1], 1))
    return got


def after(x, *others):
    return lax.optimization_barrier((x,) + others)[0]


def put(buffer, block, *starts):
    return lax.dynamic_update_slice(buffer, block.astype(buffer.dtype), starts)


def take(x, start, size, axis):
    return lax.dynamic_slice_in_dim(x, start, size, axis)


def mm(a, b, dims=((1,), (0,))):
    return lax.dot_general(a, b, (dims, ((), ())), preferred_element_type=F32)


def rms_gain(values, gain_row):
    return values * lax.rsqrt(jnp.mean(values * values, axis=-1, keepdims=True) + EPS) * gain_row


def rms_pull(values, gain_row, upstream):
    r = lax.rsqrt(jnp.mean(values * values, axis=-1, keepdims=True) + EPS)
    gu = gain_row * upstream
    mean = jnp.mean(gu * values, axis=-1, keepdims=True)
    return r * gu - values * (r * r * r * mean), jnp.sum(upstream * values * r, axis=0)


def rope_tables(offsets):
    half = HD // 2
    inverse = ROPE_BASE ** (-jnp.arange(half, dtype=F32) / half)
    angles = offsets.astype(F32)[:, None] * inverse[None, :]
    cosine, sinusoid = jnp.cos(angles), jnp.sin(angles)
    return jnp.concatenate([cosine, cosine], 1), jnp.concatenate([-sinusoid, sinusoid], 1)


def doc_info(lengths, positions):
    doc_ends = jnp.cumsum(lengths)
    passed = (doc_ends[None, :] <= positions[:, None]).astype(jnp.int32)
    doc_ids = jnp.sum(passed, axis=1)
    starts = jnp.sum(passed * lengths[None, :], axis=1)
    return doc_ids, positions - starts


def slot_table(route_rows, gate_rows, expert):
    tokens = route_rows.shape[0]
    hits = route_rows == expert
    weight_rows = jnp.sum(jnp.where(hits, gate_rows, 0.0), axis=1)
    chosen = jnp.any(hits, axis=1)
    slot_rows = jnp.cumsum(chosen.astype(jnp.int32)) - 1
    matches = (slot_rows[None, :] == jnp.arange(CAP, dtype=jnp.int32)[:, None]) & chosen[None, :]
    weights = jnp.sum(jnp.where(matches, weight_rows[None, :], 0.0), axis=1)
    return matches.astype(BF), weights[:, None]


def qkv_body(blocks, width, *refs):
    toks = refs[:blocks]
    gain, weights, qgain, kgain, cosine, sinusoid = refs[blocks : blocks + 6]
    normed_out, q_out, k_out, v_out, qraw_out, kraw_out = refs[blocks + 6 : blocks + 12]
    buf, sems = refs[blocks + 12 :]
    step = pl.program_id(0)

    @pl.when(step == 0)
    def _():
        for j in range(blocks):
            pltpu.make_async_copy(toks[j], buf.at[j], sems.at[j]).start()

    for j in range(blocks):

        @pl.when(step == j)
        def _(j=j):
            pltpu.make_async_copy(toks[j], buf.at[j], sems.at[j]).wait()

    x = buf[step].astype(F32)
    r = lax.rsqrt(jnp.mean(x * x, axis=-1, keepdims=True) + EPS)
    normed = (x * r * gain[...]).astype(BF)
    normed_out[...] = normed
    raw = mm(normed, weights[...])
    cos, sin = cosine[...], sinusoid[...]
    for out, raw_out, gains, base in ((q_out, qraw_out, qgain, 0), (k_out, kraw_out, kgain, width)):
        for start in range(0, width, HD):
            part = raw[:, base + start : base + start + HD]
            raw_out[:, start : start + HD] = part
            n = rms_gain(part, gains[...])
            out[:, start : start + HD] = (n * cos + pltpu.roll(n, HD // 2, 1) * sin).astype(BF)
    v_out[...] = raw[:, 2 * width :].astype(BF)


def qkv_call(toks, gain, weights, qgain, kgain, cosine, sinusoid):
    blocks = len(toks)
    rows, width = toks[0].shape[0], weights.shape[1] // 3
    total = rows * blocks
    whole = lambda a: pl.BlockSpec(a.shape, lambda i: (0,) * a.ndim)
    strip = lambda n: pl.BlockSpec((rows, n), lambda i: (i, 0))
    return pl.pallas_call(
        partial(qkv_body, blocks, width),
        grid=(blocks,),
        in_specs=[pl.BlockSpec(memory_space=pl.ANY)] * blocks
        + [whole(gain), whole(weights), whole(qgain), whole(kgain), strip(HD), strip(HD)],
        out_specs=[strip(D), strip(width), strip(width), strip(width), strip(width), strip(width)],
        out_shape=[
            jax.ShapeDtypeStruct((total, D), BF),
            jax.ShapeDtypeStruct((total, width), BF),
            jax.ShapeDtypeStruct((total, width), BF),
            jax.ShapeDtypeStruct((total, width), BF),
            jax.ShapeDtypeStruct((total, width), F32),
            jax.ShapeDtypeStruct((total, width), F32),
        ],
        scratch_shapes=[
            pltpu.VMEM((blocks, rows, D), BF),
            pltpu.SemaphoreType.DMA((blocks,)),
        ],
        cost_estimate=pl.CostEstimate(
            flops=2 * total * D * 3 * width,
            bytes_accessed=4 * total * D + 2 * D * 3 * width,
            transcendentals=0,
        ),
        name="qkv",
    )(*toks, gain, weights, qgain, kgain, cosine, sinusoid)


def soft_rows(q, k, query_docs, key_docs):
    scores = mm(k, q, ((1,), (1,))) * SCALE
    scores = jnp.where(key_docs == query_docs, scores, NEG)
    high = jnp.max(scores, axis=0, keepdims=True)
    terms = jnp.exp(scores - high)
    return terms * (1.0 / jnp.sum(terms, axis=0, keepdims=True))


def attend_body(q, k, v, query_docs, key_docs, out):
    chances = soft_rows(q[...], k[...], query_docs[...], key_docs[...])
    mixed = mm(v[...], chances.astype(BF), ((0,), (0,)))
    out[...] = jnp.transpose(mixed).astype(BF)


def attend_call(q, k, v, query_docs, key_docs, rows):
    total, width = q.shape
    heads = width // HD
    block = pl.BlockSpec((rows, HD), lambda h, i: (i, h))
    column = pl.BlockSpec((total, HD), lambda h, i: (0, h))
    return pl.pallas_call(
        attend_body,
        grid=(heads, total // rows),
        in_specs=[
            block,
            column,
            column,
            pl.BlockSpec((1, rows), lambda h, i: (0, i)),
            pl.BlockSpec((total, 1), lambda h, i: (0, 0)),
        ],
        out_specs=block,
        out_shape=jax.ShapeDtypeStruct((total, width), BF),
        cost_estimate=pl.CostEstimate(
            flops=4 * total * total * width,
            bytes_accessed=8 * total * width,
            transcendentals=total * total * heads,
        ),
        name="attend",
    )(q, k, v, query_docs, key_docs)


def pull_body(
    steps, q, k, v, grad, query_docs, key_docs, qraw, kraw, qgain, kgain,
    cosine, sinusoid, cosine_all, sinusoid_all, dqkv, dqg, dkg, dk_sum, dv_sum,
):
    head, step = pl.program_id(0), pl.program_id(1)
    heads = pl.num_programs(0)
    rows = q.shape[0]
    chances = soft_rows(q[...], k[...], query_docs[...], key_docs[...])
    pulled = mm(v[...], grad[...], ((1,), (1,)))
    delta = jnp.sum(chances * pulled, axis=0, keepdims=True)
    score_low = (chances * (pulled - delta)).astype(BF)
    dq = jnp.transpose(mm(k[...], score_low, ((0,), (0,)))) * SCALE
    dk = mm(score_low, q[...])
    dv = mm(chances.astype(BF), grad[...])

    @pl.when(step == 0)
    def _():
        dk_sum[...] = dk
        dv_sum[...] = dv

    @pl.when(step > 0)
    def _():
        dk_sum[...] += dk
        dv_sum[...] += dv

    @pl.when((head == 0) & (step == 0))
    def _():
        dqg[...] = jnp.zeros_like(dqg)
        dkg[...] = jnp.zeros_like(dkg)

    def through(upstream, cos, sin, raw, gain):
        turned = upstream * cos - pltpu.roll(upstream, HD // 2, 1) * sin
        return rms_pull(raw, gain, turned)

    low, gain_part = through(dq, cosine[...], sinusoid[...], qraw[...], qgain[...])
    dqg[...] += gain_part[None]
    column = lambda n: pl.ds(pl.multiple_of(n * HD, HD), HD)
    dqkv[pl.ds(pl.multiple_of(step * rows, rows), rows), column(head)] = low.astype(BF)

    @pl.when(step == steps - 1)
    def _():
        low, gain_part = through(
            dk_sum[...] * SCALE, cosine_all[...], sinusoid_all[...], kraw[...], kgain[...]
        )
        dkg[...] += gain_part[None]
        dqkv[:, column(heads + head)] = low.astype(BF)
        dqkv[:, column(2 * heads + head)] = dv_sum[...].astype(BF)


def pull_call(q, k, v, grad, query_docs, key_docs, qraw, kraw, qgain, kgain, cosine, sinusoid, rows):
    total, width = q.shape
    heads, steps = width // HD, total // rows
    block = pl.BlockSpec((rows, HD), lambda h, i: (i, h))
    column = pl.BlockSpec((total, HD), lambda h, i: (0, h))
    strip = pl.BlockSpec((rows, HD), lambda h, i: (i, 0))
    fixed = lambda r, c: pl.BlockSpec((r, c), lambda h, i: (0, 0))
    return pl.pallas_call(
        partial(pull_body, steps),
        grid=(heads, steps),
        in_specs=[
            block,
            column,
            column,
            block,
            pl.BlockSpec((1, rows), lambda h, i: (0, i)),
            fixed(total, 1),
            block,
            column,
            fixed(1, HD),
            fixed(1, HD),
            strip,
            strip,
            fixed(total, HD),
            fixed(total, HD),
        ],
        out_specs=[fixed(total, 3 * width), fixed(1, HD), fixed(1, HD)],
        out_shape=[
            jax.ShapeDtypeStruct((total, 3 * width), BF),
            jax.ShapeDtypeStruct((1, HD), F32),
            jax.ShapeDtypeStruct((1, HD), F32),
        ],
        scratch_shapes=[pltpu.VMEM((total, HD), F32), pltpu.VMEM((total, HD), F32)],
        cost_estimate=pl.CostEstimate(
            flops=10 * total * total * width,
            bytes_accessed=20 * total * width,
            transcendentals=total * total * heads,
        ),
        name="attend_pull",
    )(
        q, k, v, grad, query_docs, key_docs, qraw, kraw, qgain, kgain,
        cosine, sinusoid, cosine, sinusoid,
    )


def spread_body(blocks, places, *refs):
    parts = refs[:blocks]
    outs = refs[blocks : blocks + 3]
    buf, sems = refs[blocks + 3 :]
    step = pl.program_id(0)
    width = buf.shape[2] // 3

    @pl.when(step == 0)
    def _():
        for j in range(blocks):
            pltpu.make_async_copy(parts[j], buf.at[j], sems.at[j]).start()

    for j in range(blocks):

        @pl.when(step == j)
        def _(j=j):
            pltpu.make_async_copy(parts[j], buf.at[j], sems.at[j]).wait()

    x = buf[step].astype(F32)
    for n in range(3):
        outs[n][...] = x[:, n * width : (n + 1) * width]


def spread_call(parts, places):
    blocks = len(parts)
    rows, width = parts[0].shape[0], parts[0].shape[1] // 3
    return pl.pallas_call(
        lambda places, *refs: spread_body(blocks, places, *refs),
        grid_spec=pltpu.PrefetchScalarGridSpec(
            num_scalar_prefetch=1,
            grid=(blocks,),
            in_specs=[pl.BlockSpec(memory_space=pl.ANY)] * blocks,
            out_specs=[pl.BlockSpec((rows, width), lambda i, places: (0, places[i]))] * 3,
            scratch_shapes=[
                pltpu.VMEM((blocks, rows, 3 * width), BF),
                pltpu.SemaphoreType.DMA((blocks,)),
            ],
        ),
        out_shape=[jax.ShapeDtypeStruct((rows, blocks * width), F32)] * 3,
        name="spread",
    )(places, *parts)


def per_device(
    tokens, out_grad, doc_lengths, routes, gate_values, attn_gain, w_query, w_key, w_value, w_out,
    query_gain, key_gain, ffn_gain, w_gate, w_up, w_down,
):
    fs, cs = lax.axis_size("fsdp"), lax.axis_size("ctx")
    zs = cs // 2
    assert fs & (fs - 1) == 0 and cs % 2 == 0 and HEADS % cs == 0
    f, c = lax.axis_index("fsdp"), lax.axis_index("ctx")
    z, h = c // 2, c % 2
    micros, count = tokens.shape[0], tokens.shape[2]
    total = count * cs
    width = HEADS // cs * HD
    rows_f = D // fs
    ff = w_gate.shape[2]
    ff_f = ff // fs
    query_rows = min(256, total)
    others = range(1, fs)

    small = jnp.concatenate([attn_gain, ffn_gain, query_gain, key_gain])[None]
    gains = jnp.zeros((fs, small.shape[1]), BF)
    gains = put(gains, small, f, 0)
    for k in others:
        gains = put(gains, fx(small, k), f ^ k, 0)
    gains = gains.astype(F32)
    attn_gains = gains[:, :rows_f].reshape(1, D)
    ffn_gains = gains[:, rows_f : 2 * rows_f].reshape(1, D)
    query_gains = gains[:, 2 * rows_f : 2 * rows_f + HD // fs].reshape(1, HD)
    key_gains = gains[:, 2 * rows_f + HD // fs :].reshape(1, HD)

    own = jnp.concatenate([take(w, c * width, width, 1) for w in (w_query, w_key, w_value)], 1)
    came = [fx(own, k) for k in others]
    w_qkv = put(jnp.zeros((D, 3 * width), BF), own, f * rows_f, 0)
    for k in others:
        w_qkv = put(w_qkv, came[k - 1], (f ^ k) * rows_f, 0)

    half_rows = rows_f // 2
    half = after(take(w_out, h * half_rows, half_rows, 0), *came)
    halves = [fx(half, k) for k in others]
    w_out_all = put(jnp.zeros((D, D), BF), w_out, f * rows_f, 0)
    for k in others:
        w_out_all = put(w_out_all, halves[k - 1], (f ^ k) * rows_f + h * half_rows, 0)
        w_out_all = put(w_out_all, swap(halves[k - 1]), (f ^ k) * rows_f + (1 - h) * half_rows, 0)

    origin = jnp.stack(
        [((z - k) % zs) * 2 + (h ^ e) for k in range(zs) for e in range(2)]
    ).astype(jnp.int32)
    positions = (origin[:, None] * count + jnp.arange(count, dtype=jnp.int32)[None]).reshape(-1)

    state = []
    previous = []
    for m in range(micros):
        ring = zring(after(tokens[m, 0], *previous))
        previous = ring[-1:]
        toks = [b for block in ring for b in (block, swap(block))]
        docs, offsets = doc_info(doc_lengths[m, 0], positions)
        cosine, sinusoid = rope_tables(offsets)
        state.append(dict(toks=toks, row=docs[None, :], col=docs[:, None], cos=cosine, sin=sinusoid))

    for m in range(micros):
        s = state[m]
        s["hot"], s["weight"] = slot_table(routes[m, 0], gate_values[m, 0], 0)
        picked = mm(s["hot"], out_grad[m, 0])
        s["out_low"] = (s["weight"] * picked).astype(BF)

    hidden_parts = []
    for m in range(micros):
        s = state[m]
        s["normed"], s["q"], s["k"], s["v"], s["qraw"], s["kraw"] = qkv_call(
            s["toks"], attn_gains, w_qkv, query_gains, key_gains, s["cos"], s["sin"]
        )
        att = attend_call(s["q"], s["k"], s["v"], s["row"], s["col"], query_rows)
        att = att.reshape(zs, 2, count, width)
        mine, theirs = att[:, 0], swap(att[:, 1])
        low = jnp.where(h == 0, mine, theirs)
        high = jnp.where(h == 0, theirs, mine)
        pairs = jnp.concatenate([low, high], axis=2)
        mixed = jnp.zeros((count, D), BF)
        for k in range(zs):
            block = pairs[k] if k == 0 else zshift(pairs[k], -k)
            mixed = put(mixed, block, 0, ((z + k) % zs) * 2 * width)
        s["mixed"] = mixed
        s["hidden"] = tokens[m, 0].astype(F32) + mm(mixed, w_out_all)

    for m in range(micros):
        s = state[m]
        hidden, hot = s["hidden"], s["hot"]
        ffn_low = rms_gain(hidden, ffn_gains).astype(BF)
        slots = mm(hot, ffn_low).astype(BF)
        xs = [take(slots, f * rows_f, rows_f, 1)]
        xs += [fx(take(slots, (f ^ k) * rows_f, rows_f, 1), k) for k in others]
        x = jnp.concatenate(xs, 0)
        act = jnp.stack([mm(x, w_gate[0]), mm(x, w_up[0])])
        part = lambda k: take(act, (f ^ k) * ff_f, ff_f, 2)
        act_own = part(0)
        for k in others:
            got = fx(part(k).astype(BF), k).reshape(2, fs, CAP, ff_f)
            got = jnp.stack([got[:, b ^ k] for b in range(fs)], 1)
            act_own = act_own + got.reshape(2, fs * CAP, ff_f).astype(F32)
        gate_act, up_act = act_own[0], act_own[1]
        sig = 1.0 / (1.0 + jnp.exp(-gate_act))
        silu = gate_act * sig
        inner_low = (silu * up_act).astype(BF)
        outs = mm(inner_low, w_down[0]).reshape(fs, CAP, D)
        expert_out = outs[0]
        for k in others:
            expert_out = expert_out + fx(outs[k].astype(BF), k).astype(F32)
        weighted = (s["weight"] * expert_out).astype(BF)
        s["result"] = (hidden + mm(hot, weighted, ((0,), (0,)))).astype(BF)
        out_low = s["out_low"]
        outs_low = jnp.concatenate([out_low] + [fx(out_low, k) for k in others], 0)
        inner_grad = mm(outs_low, w_down[0], ((1,), (1,)))
        gate_low = (inner_grad * up_act * sig * (1.0 + gate_act * (1.0 - sig))).astype(BF)
        up_low = (inner_grad * silu).astype(BF)
        act_low = jnp.stack([gate_low, up_low])
        act_all = put(jnp.zeros((2, fs * CAP, ff), BF), act_low, 0, 0, f * ff_f)
        for k in others:
            got = fx(act_low, k).reshape(2, fs, CAP, ff_f)
            got = jnp.stack([got[:, b ^ k] for b in range(fs)], 1)
            act_all = put(act_all, got.reshape(2, fs * CAP, ff_f), 0, 0, (f ^ k) * ff_f)
        rows_grad = mm(act_all[0], w_gate[0], ((1,), (1,))) + mm(act_all[1], w_up[0], ((1,), (1,)))
        rows_low = rows_grad.astype(BF).reshape(fs, CAP, rows_f)
        slots_grad = put(jnp.zeros((CAP, D), BF), rows_low[0], 0, f * rows_f)
        for k in others:
            slots_grad = put(slots_grad, fx(rows_low[k], k), 0, (f ^ k) * rows_f)
        ffn_grad = mm(hot, slots_grad, ((0,), (0,)))
        part_grad, s["ffn_gain_grad"] = rms_pull(hidden, ffn_gains, ffn_grad)
        s["hidden_grad"] = out_grad[m, 0].astype(F32) + part_grad
        s["branch_low"] = s["hidden_grad"].astype(BF)
        s["x"], s["act_all"], s["inner_low"], s["outs_low"] = x, act_all, inner_low, outs_low
        mixed_grad = mm(s["branch_low"], w_out_all, ((1,), (1,))).astype(BF)
        blocks = []
        for k in range(zs):
            block = take(mixed_grad, ((z + k) % zs) * 2 * width, 2 * width, 1)
            blocks.append(block if k == 0 else zshift(block, k))
        blocks = jnp.stack(blocks)
        first, second = blocks[:, :, :width], blocks[:, :, width:]
        mine = jnp.where(h == 0, first, second)
        theirs = swap(jnp.where(h == 0, second, first))
        s["mixed_grad"] = jnp.stack([mine, theirs], 1).reshape(total, width)

    both = lambda name, axis=0: jnp.concatenate([s[name] for s in state], axis)

    x, act_all, inner_low, outs_low = both("x"), both("act_all", 1), both("inner_low"), both("outs_low")
    gate_up = jnp.concatenate(
        [mm(x, act_all[0], ((0,), (0,))), mm(x, act_all[1], ((0,), (0,)))], 1
    )
    down = mm(inner_low, outs_low, ((0,), (0,))).reshape(ff_f * D // (2 * ff), 2 * ff)
    flat = jnp.concatenate([gate_up.astype(BF), down.astype(BF)], 0)
    flat = flat.reshape(2, flat.shape[0] // 2, flat.shape[1])
    flat = take(flat, h, 1, 0)[0].astype(F32) + swap(take(flat, 1 - h, 1, 0)[0]).astype(F32)

    out_part = mm(both("mixed"), both("branch_low"), ((0,), (0,))).astype(BF)
    out_part = out_part.reshape(fs, 2, half_rows, D)
    out_part = take(out_part, h, 1, 1)[:, 0].astype(F32) + swap(take(out_part, 1 - h, 1, 1)[:, 0])
    out_part = out_part.astype(BF)
    out_sum = take(out_part, f, 1, 0)[0].astype(F32)
    for k in others:
        out_sum = out_sum + fx(take(out_part, f ^ k, 1, 0)[0], k).astype(F32)

    def over_z(x):
        rows = x.shape[0] // zs
        low = x.astype(BF)
        summed = take(x, z * rows, rows, 0)
        for k in range(1, zs):
            summed = summed + zshift(take(low, ((z + k) % zs) * rows, rows, 0), k).astype(F32)
        return zring(summed.astype(BF))

    def whole(parts):
        rows, columns = parts[0].shape
        result = jnp.zeros((2 * zs * rows, columns), F32)
        for k, part in enumerate(parts):
            at = ((z - k) % zs) * rows
            result = put(result, part, h * zs * rows + at, 0)
            result = put(result, swap(part), (1 - h) * zs * rows + at, 0)
        return result

    qkv_sum = None
    query_gain_grad = key_gain_grad = 0.0
    grads = []
    for m in range(micros):
        s = state[m]
        dqkv, dqg, dkg = pull_call(
            s["q"], s["k"], s["v"], s["mixed_grad"], s["row"], s["col"], s["qraw"], s["kraw"],
            query_gains, key_gains, s["cos"], s["sin"], query_rows,
        )
        query_gain_grad, key_gain_grad = query_gain_grad + dqg[0], key_gain_grad + dkg[0]
        normed_part = mm(dqkv, w_qkv, ((1,), (1,))).astype(BF).reshape(zs, 2, count, D)
        paired = normed_part[:, 0].astype(F32) + swap(normed_part[:, 1]).astype(F32)
        normed_grad = paired[0]
        for k in range(1, zs):
            normed_grad = normed_grad + zshift(paired[k].astype(BF), -k).astype(F32)
        grads.append(normed_grad)
        part = mm(s["normed"], dqkv, ((0,), (0,)))
        qkv_sum = part if qkv_sum is None else qkv_sum + part

    qkv_low = qkv_sum.astype(BF)
    qkv_grad = take(qkv_sum, f * rows_f, rows_f, 0)
    for k in others:
        qkv_grad = qkv_grad + fx(take(qkv_low, (f ^ k) * rows_f, rows_f, 0), k).astype(F32)
    ring = zring(qkv_grad.astype(BF))
    parts = [b for block in ring for b in (block, swap(block))]
    query_grad, key_grad, value_grad = spread_call(parts, origin)

    out_grad_rows = whole(over_z(out_sum))
    flat = whole(over_z(flat))
    gate_grad, up_grad = flat[:rows_f, :ff], flat[:rows_f, ff:]
    down_grad = flat[rows_f:].reshape(ff_f, D)

    input_grads, attn_gain_grad = [], 0.0
    for m in range(micros):
        part, gain_part = rms_pull(tokens[m, 0].astype(F32), attn_gains, grads[m])
        attn_gain_grad = attn_gain_grad + gain_part
        input_grads.append(state[m]["hidden_grad"] + part)

    ffn_gain_grad = sum(s["ffn_gain_grad"] for s in state)
    sums = jnp.concatenate([attn_gain_grad, ffn_gain_grad, query_gain_grad, key_gain_grad])[None]
    sums = sums + swap(sums)
    ring = sums
    for k in range(1, zs):
        ring = ring + zshift(sums, k)
    sums = ring
    for bit in range(fs.bit_length() - 1):
        sums = sums + fx(sums, 1 << bit)
    sums = sums[0]
    shard = lambda start, size: take(sums, start + f * (size // fs), size // fs, 0)

    return (
        jnp.stack([s["result"] for s in state])[:, None],
        jnp.stack(input_grads)[:, None],
        shard(0, D),
        query_grad,
        key_grad,
        value_grad,
        out_grad_rows,
        shard(2 * D, HD),
        shard(2 * D + HD, HD),
        shard(D, D),
        gate_grad[None],
        up_grad[None],
        down_grad[None],
    )


def solution(mesh):
    activation = P(None, "fsdp", "ctx", None)
    rows, row_pairs, middle = P("fsdp"), P("fsdp", None), P(None, "fsdp", None)
    in_specs = (
        activation, activation, P(None, "fsdp", None), activation, activation,
        rows, row_pairs, row_pairs, row_pairs, row_pairs, rows, rows, rows, middle, middle, middle,
    )
    out_specs = (
        activation, activation, rows, row_pairs, row_pairs, row_pairs, row_pairs,
        rows, rows, rows, middle, middle, middle,
    )
    return jax.shard_map(
        per_device, mesh=mesh, in_specs=in_specs, out_specs=out_specs, check_vma=False
    )
```
